1024 devices in a mesh: fsdp: 32 (over z_hi, x, core), ctx: 32 (over y, z_lo).
Axes of the slice: x: 4, y: 4, z: 32 (z_hi: 4, z_lo: 8; z = z_hi * 8 + z_lo), core: 2. Of those that a mesh axis runs over, the one named last changes fastest.
Arguments:
- queries: bfloat16 [32, 4096, 2048], P('fsdp', 'ctx'), may hold values from -200 to 200
- keyvals: bfloat16 [32, 4096, 2, 512], P('fsdp', 'ctx'), may hold values from -6 to 6
- span_ids: int32 [32, 64], P('fsdp'), may hold values from 0 to 63, as said below
Outputs:
- attended: bfloat16 [32, 4096, 2048], P('fsdp', 'ctx')
The draws below stay inside these ranges and needn't reach their ends.
Inputs may be any that keep to these rules, and one draw needn't show every extreme that they name: `span_ids`: in each sequence, ctx device d holds storage spans 2d and 2d+1; storage span 2d has position span p with p < 32 and storage span 2d+1 has position span 64 - 1-p; each p belongs to exactly one device.
All inputs are finite; a program needn't handle non-finite values.
Results may differ from the reference program's by a relative error of at most 0.0041.
Values may be sent and summed in bfloat16 or wider, within the bound.
A program may use at most 64 MiB of HBM per device.

```python
import math
import jax
import jax.numpy as jnp
from jax import lax

KV_HEADS = 4
GROUP = 4
HEAD_DIM = 128
SPAN = 64
SPANS = 64
SEQ = 4096
SEQS = 32


def shared_keyvals(key):
    base = jax.random.fold_in(key, 11)
    values = jax.random.normal(base, (SEQS, SEQ, 2, KV_HEADS * HEAD_DIM), jnp.float32)
    return jnp.clip(values, -6.0, 6.0)


def draw_keyvals(key, part):
    return shared_keyvals(key).astype(jnp.bfloat16)


def draw_queries(key, part):
    base = jax.random.fold_in(key, 23)
    width = KV_HEADS * GROUP * HEAD_DIM
    drawn = jax.random.normal(base, (SEQS, SEQ, width), jnp.float32)
    return jnp.clip(drawn, -200.0, 200.0).astype(jnp.bfloat16)


def draw_span_ids(key, part):
    half_count = SPANS // 2
    keys = jax.random.split(jax.random.fold_in(key, 37), SEQS)
    orders = jax.vmap(lambda one_key: jax.random.permutation(one_key, half_count))(keys).astype(jnp.int32)
    mirrored = (SPANS - 1 - orders).astype(jnp.int32)
    return jnp.stack([orders, mirrored], axis=-1).reshape(SEQS, SPANS).astype(jnp.int32)


def setup_inputs(seed: int = 0) -> dict:
    seeds = jax.random.split(jax.random.key(seed), 4)
    return {
        "queries": draw_queries(jax.random.fold_in(seeds[3], 71), 0),
        "keyvals": draw_keyvals(jax.random.fold_in(seeds[3], 71), 0),
        "span_ids": draw_span_ids(jax.random.fold_in(seeds[3], 71), 0),
    }


def attend(query_seq, keyval_seq, span_table):
    offsets = jnp.arange(SPAN, dtype=jnp.int32)
    positions = (span_table[:, None] * SPAN + offsets[None, :]).reshape(-1).astype(jnp.int32)
    keys = keyval_seq[:, 0].reshape(SEQ, KV_HEADS, HEAD_DIM).astype(jnp.float32)
    values = keyval_seq[:, 1].reshape(SEQ, KV_HEADS, HEAD_DIM).astype(jnp.float32)
    block_rows = math.gcd(SEQ, 512)
    block_count = SEQ // block_rows
    query_blocks = query_seq.reshape(block_count, block_rows, KV_HEADS, GROUP, HEAD_DIM)
    pos_blocks = positions.reshape(block_count, block_rows)
    scale = 1.0 / math.sqrt(HEAD_DIM)

    def one_block(pair):
        query_block, query_pos = pair
        scores = jnp.einsum('qhgd,khd->hgqk', query_block.astype(jnp.float32), keys) * scale
        allowed = positions[None, None, None, :] <= query_pos[None, None, :, None]
        scores = jnp.where(allowed, scores, -1e+30)
        highest = lax.optimization_barrier(jnp.max(scores, axis=-1, keepdims=True))
        weights = jnp.where(allowed, jnp.exp(scores - highest), 0.0)
        total = lax.optimization_barrier(jnp.sum(weights, axis=-1))
        rounded = weights.astype(jnp.bfloat16).astype(jnp.float32)
        summed = jnp.einsum('hgqk,khd->qhgd', rounded, values)
        result = summed / jnp.transpose(total, (2, 0, 1))[..., None]
        return result.reshape(block_rows, KV_HEADS * GROUP * HEAD_DIM).astype(jnp.bfloat16)
    outputs = lax.map(one_block, (query_blocks, pos_blocks))
    return outputs.reshape(SEQ, KV_HEADS * GROUP * HEAD_DIM)

def reference(queries, keyvals, span_ids):
    attended = lax.map(lambda triple: attend(triple[0], triple[1], triple[2]), (queries, keyvals, span_ids))
    return attended
```

```python
import functools
import math

import jax
import jax.numpy as jnp
from jax import lax
from jax.experimental import pallas as pl
from jax.experimental.pallas import tpu as pltpu
from jax.sharding import PartitionSpec as P

HEADS = 4
GROUP = 4
DIM = 128
SPAN = 64
ROWS = 2 * SPAN
NEG = -1e30
MESH = pl.DeviceIdType.MESH
FACTOR = math.log2(math.e) / math.sqrt(DIM)


def gray(j):
    return j + (j // 2) * (5 - 2 * j)


def kernel(
    nz, ids_ref, q_ref, kv_ref, out_ref,
    kv_buf, q_buf, o_buf, gap, acc, total, top,
    recv, right_sem, left_sem, kv_sem, q_sem, q_recv, o_sem, o_recv, own_sem,
):
    me = lax.axis_index("ctx")
    y, z = me // nz, me % nz
    has_left, has_right = z > 0, z < nz - 1
    width = GROUP * DIM
    keys = HEADS * SPAN

    def device(yy, zz):
        return {"ctx": yy * nz + zz}

    def remote(src, dst, send, receive, where):
        return pltpu.make_async_remote_copy(
            src_ref=src, dst_ref=dst, send_sem=send, recv_sem=receive,
            device_id=where, device_id_type=MESH,
        )

    def piece(zz, yy):
        return kv_buf.at[zz, :, :, yy]

    def columns(yy):
        return pl.ds(pl.multiple_of(yy * width, width), width)

    def other(d):
        return (y + d) % HEADS

    barrier = pltpu.get_barrier_semaphore()
    for d in (1, 2, 3):
        pl.semaphore_signal(barrier, inc=1, device_id=device(other(d), z), device_id_type=MESH)

    @pl.when(has_left)
    def _():
        pl.semaphore_signal(barrier, inc=1, device_id=device(y, z - 1), device_id_type=MESH)

    @pl.when(has_right)
    def _():
        pl.semaphore_signal(barrier, inc=1, device_id=device(y, z + 1), device_id_type=MESH)

    pl.semaphore_wait(barrier, 3 + (z + nz - 1) // nz + (2 * nz - 2 - z) // nz)

    def to_right(src, zz, yy):
        return remote(src, piece(zz, yy), right_sem.at[zz, yy], recv.at[zz, yy], device(y, z + 1))

    def to_left(src, zz, yy):
        return remote(src, piece(zz, yy), left_sem.at[zz, yy], recv.at[zz, yy], device(y, z - 1))

    def arrived(zz, yy):
        remote(piece(zz, yy), piece(zz, yy), recv.at[zz, yy], recv.at[zz, yy], device(y, z)).wait_recv()

    @pl.when(has_right)
    def _():
        to_right(kv_ref.at[y], z, y).start()

    @pl.when(has_left)
    def _():
        to_left(kv_ref.at[y], z, y).start()

    kv_sends = [
        remote(kv_ref.at[other(d)], piece(z, y), kv_sem.at[d - 1], recv.at[z, y], device(other(d), z))
        for d in (1, 3, 2)
    ]
    for copy in kv_sends:
        copy.start()
    own_kv = pltpu.make_async_copy(kv_ref.at[y], piece(z, y), own_sem.at[0])
    own_kv.start()
    q_sends = [
        remote(
            q_ref.at[:, columns(other(d))], q_buf.at[y], q_sem.at[d - 1], q_recv.at[y], device(other(d), z)
        )
        for d in (1, 3, 2)
    ]
    for copy in q_sends:
        copy.start()
    own_q = pltpu.make_async_copy(q_ref.at[:, columns(y)], q_buf.at[y], own_sem.at[1])
    own_q.start()

    for d in (1, 3, 2):
        arrived(z, other(d))

        @pl.when(has_right)
        def _():
            to_right(piece(z, other(d)), z, other(d)).start()

        @pl.when(has_left)
        def _():
            to_left(piece(z, other(d)), z, other(d)).start()

    lane = lax.broadcasted_iota(jnp.int32, (SPAN, keys), 1)
    row = lax.broadcasted_iota(jnp.int32, (SPAN, keys), 0)
    base = lane % SPAN - row

    def fill(zz, carry):
        for half in range(2):
            span = jnp.zeros((SPAN, keys), jnp.int32)
            for yy in range(HEADS):
                span = jnp.where(lane // SPAN == yy, ids_ref[0, 2 * (yy * nz + zz) + half], span)
            gap[zz, half] = span * SPAN + base
        return carry

    lax.fori_loop(0, nz, fill, 0)
    top[...] = jnp.full(top.shape, NEG, jnp.float32)
    total[...] = jnp.zeros(total.shape, jnp.float32)
    acc[...] = jnp.zeros(acc.shape, jnp.float32)
    own_kv.wait()
    own_q.wait()

    def product(a, b):
        return lax.dot_general(a, b, (((1,), (1,)), ((), ())), preferred_element_type=jnp.float32)

    def update(yq, rows, scores, values):
        best = scores[0]
        for s in scores[1:]:
            best = jnp.maximum(best, s)
        old = top[yq, rows]
        new = jnp.maximum(old, jnp.max(best, axis=-1, keepdims=True))
        shrink = jnp.exp2((old - new) * FACTOR)
        wide = jnp.concatenate([new] * (keys // DIM), axis=-1)
        weighted = acc[yq, rows] * shrink
        summed = total[yq, rows] * shrink
        for s, v in zip(scores, values):
            p = jnp.exp2((s - wide) * FACTOR)
            for k in range(keys // DIM):
                summed = summed + p[:, k * DIM : (k + 1) * DIM]
            weighted = weighted + jnp.dot(p.astype(jnp.bfloat16), v, preferred_element_type=jnp.float32)
        acc[yq, rows] = weighted
        total[yq, rows] = summed
        top[yq, rows] = new

    def attend(yq, zz):
        low_k, high_k, low_v, high_v = (
            kv_buf[zz, a, b].reshape(keys, DIM) for a in range(2) for b in range(2)
        )
        low_q, high_q = (
            jnp.concatenate(
                [q_buf[yq, b * SPAN : (b + 1) * SPAN, g * DIM : (g + 1) * DIM] for g in range(GROUP)], axis=0
            )
            for b in range(2)
        )
        home = 2 * (yq * nz + z)

        def masked(s, half):
            distance = jnp.concatenate([gap[zz, half]] * GROUP, axis=0)
            return jnp.where(distance <= ids_ref[0, home + half] * SPAN, s, NEG)

        half_rows = GROUP * SPAN
        update(yq, pl.ds(0, half_rows), [masked(product(low_q, low_k), 0)], [low_v])
        update(
            yq, pl.ds(half_rows, half_rows),
            [product(high_q, low_k), masked(product(high_q, high_k), 1)], [low_v, high_v],
        )

    def both_sides(yq, step):
        @pl.when(z - step >= 0)
        def _():
            attend(yq, z - step)

        @pl.when(jnp.logical_and(z + step < nz, step > 0))
        def _():
            attend(yq, z + step)

    def advance(step, carry):
        def part(j, inner):
            yy = other(gray(j))

            @pl.when(z - step >= 0)
            def _():
                arrived(z - step, yy)

                @pl.when(has_right)
                def _():
                    to_right(piece(z - step, yy), z - step, yy).start()

            @pl.when(z + step < nz)
            def _():
                arrived(z + step, yy)

                @pl.when(has_left)
                def _():
                    to_left(piece(z + step, yy), z + step, yy).start()

            @pl.when(jnp.logical_and(step == 1, j > 0))
            def _():
                remote(q_buf.at[yy], q_buf.at[yy], q_recv.at[yy], q_recv.at[yy], device(y, z)).wait_recv()

            both_sides(yy, step - 1)
            return inner

        return lax.fori_loop(0, HEADS, part, carry)

    lax.fori_loop(1, nz, advance, 0)

    def finish(j, carry):
        yq = other(gray(HEADS - 1 - j))
        both_sides(yq, nz - 1)
        out = acc[yq] / jnp.sum(total[yq], axis=-1, keepdims=True)
        out = out.astype(jnp.bfloat16)
        for b in range(2):
            for g in range(GROUP):
                start = (b * GROUP + g) * SPAN
                o_buf[yq, b * SPAN : (b + 1) * SPAN, g * DIM : (g + 1) * DIM] = out[start : start + SPAN]

        @pl.when(j < HEADS - 1)
        def _():
            remote(
                o_buf.at[yq], out_ref.at[:, columns(y)], o_sem.at[yq], o_recv.at[y], device(yq, z)
            ).start()

        return carry

    lax.fori_loop(0, HEADS, finish, 0)
    own_o = pltpu.make_async_copy(o_buf.at[y], out_ref.at[:, columns(y)], own_sem.at[2])
    own_o.start()

    for copy in kv_sends + q_sends:
        copy.wait_send()

    def drain(yy, carry):
        @pl.when(has_right)
        def _():
            def one(zz, inner):
                to_right(piece(zz, yy), zz, yy).wait_send()
                return inner

            lax.fori_loop(0, z + 1, one, 0)

        @pl.when(has_left)
        def _():
            def one(zz, inner):
                to_left(piece(zz, yy), zz, yy).wait_send()
                return inner

            lax.fori_loop(z, nz, one, 0)

        return carry

    lax.fori_loop(0, HEADS, drain, 0)
    for d in (1, 2, 3):
        yy = other(d)
        copy = remote(o_buf.at[yy], out_ref.at[:, columns(yy)], o_sem.at[yy], o_recv.at[yy], device(yy, z))
        copy.wait_send()
        copy.wait_recv()
    own_o.wait()


def per_device(queries, keyvals, span_ids):
    nz = lax.axis_size("ctx") // HEADS
    q = queries[0]
    kv = keyvals[0].reshape(2, SPAN, 2, HEADS, DIM).transpose(3, 2, 0, 1, 4)
    rows = 2 * GROUP * SPAN
    dma = pltpu.SemaphoreType.DMA
    flops = 4 * HEADS * rows * DIM * nz * HEADS * ROWS
    out = pl.pallas_call(
        functools.partial(kernel, nz),
        out_shape=jax.ShapeDtypeStruct(q.shape, jnp.bfloat16),
        in_specs=[
            pl.BlockSpec(memory_space=pltpu.SMEM),
            pl.BlockSpec(memory_space=pl.ANY),
            pl.BlockSpec(memory_space=pl.ANY),
        ],
        out_specs=pl.BlockSpec(memory_space=pl.ANY),
        scratch_shapes=[
            pltpu.VMEM((nz, 2, 2, HEADS, SPAN, DIM), jnp.bfloat16),
            pltpu.VMEM((HEADS, ROWS, GROUP * DIM), jnp.bfloat16),
            pltpu.VMEM((HEADS, ROWS, GROUP * DIM), jnp.bfloat16),
            pltpu.VMEM((nz, 2, SPAN, HEADS * SPAN), jnp.int32),
            pltpu.VMEM((HEADS, rows, DIM), jnp.float32),
            pltpu.VMEM((HEADS, rows, DIM), jnp.float32),
            pltpu.VMEM((HEADS, rows, DIM), jnp.float32),
            dma((nz, HEADS)), dma((nz, HEADS)), dma((nz, HEADS)),
            dma((3,)), dma((3,)), dma((HEADS,)), dma((HEADS,)), dma((HEADS,)), dma((3,)),
        ],
        compiler_params=pltpu.CompilerParams(
            collective_id=0, has_side_effects=True, vmem_limit_bytes=48 * 1024 * 1024
        ),
        cost_estimate=pl.CostEstimate(flops=flops, bytes_accessed=4 * 1024 * 1024, transcendentals=0),
        name="attend",
    )(span_ids, q, kv)
    return out[None]


def solution(mesh):
    in_specs = (P("fsdp", "ctx", None), P("fsdp", "ctx", None, None), P("fsdp", None))
    return jax.shard_map(
        per_device, mesh=mesh, in_specs=in_specs, out_specs=P("fsdp", "ctx", None), check_vma=False
    )
```

```python
import functools
import math

import jax
import jax.numpy as jnp
from jax import lax
from jax.experimental import pallas as pl
from jax.experimental.pallas import tpu as pltpu
from jax.sharding import PartitionSpec as P

HEADS = 4
GROUP = 4
DIM = 128
SPAN = 64
ROWS = 2 * SPAN
NEG = -1e30
MESH = pl.DeviceIdType.MESH
FACTOR = math.log2(math.e) / math.sqrt(DIM)


def gray(j):
    return j + (j // 2) * (5 - 2 * j)


def kernel(
    nz, ids_ref, q_ref, kv_ref, out_ref,
    kv_buf, q_buf, o_buf, gap, acc, total, top,
    recv, right_sem, left_sem, kv_sem, q_sem, q_recv, o_sem, o_recv, own_sem,
):
    me = lax.axis_index("ctx")
    y, z = me // nz, me % nz
    has_left, has_right = z > 0, z < nz - 1
    width = GROUP * DIM
    keys = HEADS * SPAN

    def device(yy, zz):
        return {"ctx": yy * nz + zz}

    def remote(src, dst, send, receive, where):
        return pltpu.make_async_remote_copy(
            src_ref=src, dst_ref=dst, send_sem=send, recv_sem=receive,
            device_id=where, device_id_type=MESH,
        )

    def piece(zz, yy):
        return kv_buf.at[zz, :, :, yy]

    def columns(yy):
        return pl.ds(pl.multiple_of(yy * width, width), width)

    def other(d):
        return (y + d) % HEADS

    barrier = pltpu.get_barrier_semaphore()
    for d in (1, 2, 3):
        pl.semaphore_signal(barrier, inc=1, device_id=device(other(d), z), device_id_type=MESH)

    @pl.when(has_left)
    def _():
        pl.semaphore_signal(barrier, inc=1, device_id=device(y, z - 1), device_id_type=MESH)

    @pl.when(has_right)
    def _():
        pl.semaphore_signal(barrier, inc=1, device_id=device(y, z + 1), device_id_type=MESH)

    pl.semaphore_wait(barrier, 3 + (z + nz - 1) // nz + (2 * nz - 2 - z) // nz)

    def to_right(src, zz, yy):
        return remote(src, piece(zz, yy), right_sem.at[zz, yy], recv.at[zz, yy], device(y, z + 1))

    def to_left(src, zz, yy):
        return remote(src, piece(zz, yy), left_sem.at[zz, yy], recv.at[zz, yy], device(y, z - 1))

    def arrived(zz, yy):
        remote(piece(zz, yy), piece(zz, yy), recv.at[zz, yy], recv.at[zz, yy], device(y, z)).wait_recv()

    @pl.when(has_right)
    def _():
        to_right(kv_ref.at[y], z, y).start()

    @pl.when(has_left)
    def _():
        to_left(kv_ref.at[y], z, y).start()

    kv_sends = [
        remote(kv_ref.at[other(d)], piece(z, y), kv_sem.at[d - 1], recv.at[z, y], device(other(d), z))
        for d in (1, 3, 2)
    ]
    for copy in kv_sends:
        copy.start()
    own_kv = pltpu.make_async_copy(kv_ref.at[y], piece(z, y), own_sem.at[0])
    own_kv.start()
    q_sends = [
        remote(
            q_ref.at[:, columns(other(d))], q_buf.at[y], q_sem.at[d - 1], q_recv.at[y], device(other(d), z)
        )
        for d in (1, 3, 2)
    ]
    for copy in q_sends:
        copy.start()
    own_q = pltpu.make_async_copy(q_ref.at[:, columns(y)], q_buf.at[y], own_sem.at[1])
    own_q.start()

    for d in (1, 3, 2):
        arrived(z, other(d))

        @pl.when(has_right)
        def _():
            to_right(piece(z, other(d)), z, other(d)).start()

        @pl.when(has_left)
        def _():
            to_left(piece(z, other(d)), z, other(d)).start()

    lane = lax.broadcasted_iota(jnp.int32, (SPAN, keys), 1)
    row = lax.broadcasted_iota(jnp.int32, (SPAN, keys), 0)
    base = lane % SPAN - row

    def fill(zz, carry):
        for half in range(2):
            span = jnp.zeros((SPAN, keys), jnp.int32)
            for yy in range(HEADS):
                span = jnp.where(lane // SPAN == yy, ids_ref[0, 2 * (yy * nz + zz) + half], span)
            gap[zz, half] = span * SPAN + base
        return carry

    lax.fori_loop(0, nz, fill, 0)
    top[...] = jnp.full(top.shape, NEG, jnp.float32)
    total[...] = jnp.zeros(total.shape, jnp.float32)
    acc[...] = jnp.zeros(acc.shape, jnp.float32)
    own_kv.wait()
    own_q.wait()

    def product(a, b):
        return lax.dot_general(a, b, (((1,), (1,)), ((), ())), preferred_element_type=jnp.float32)

    def update(yq, rows, scores, values):
        best = scores[0]
        for s in scores[1:]:
            best = jnp.maximum(best, s)
        old = top[yq, rows]
        new = jnp.maximum(old, jnp.max(best, axis=-1, keepdims=True))
        shrink = jnp.exp2((old - new) * FACTOR)
        wide = jnp.concatenate([new] * (keys // DIM), axis=-1)
        weighted = acc[yq, rows] * shrink
        summed = total[yq, rows] * shrink
        for s, v in zip(scores, values):
            p = jnp.exp2((s - wide) * FACTOR)
            for k in range(keys // DIM):
                summed = summed + p[:, k * DIM : (k + 1) * DIM]
            weighted = weighted + jnp.dot(p.astype(jnp.bfloat16), v, preferred_element_type=jnp.float32)
        acc[yq, rows] = weighted
        total[yq, rows] = summed
        top[yq, rows] = new

    def attend(yq, zz):
        low_k, high_k, low_v, high_v = (
            kv_buf[zz, a, b].reshape(keys, DIM) for a in range(2) for b in range(2)
        )
        low_q, high_q = (
            jnp.concatenate(
                [q_buf[yq, b * SPAN : (b + 1) * SPAN, g * DIM : (g + 1) * DIM] for g in range(GROUP)], axis=0
            )
            for b in range(2)
        )
        home = 2 * (yq * nz + z)

        def masked(s, half):
            distance = jnp.concatenate([gap[zz, half]] * GROUP, axis=0)
            return jnp.where(distance <= ids_ref[0, home + half] * SPAN, s, NEG)

        half_rows = GROUP * SPAN
        update(yq, pl.ds(0, half_rows), [masked(product(low_q, low_k), 0)], [low_v])
        update(
            yq, pl.ds(half_rows, half_rows),
            [product(high_q, low_k), masked(product(high_q, high_k), 1)], [low_v, high_v],
        )

    rightward = (3 * nz - 2 - 2 * z) // (2 * nz)
    shorter = rightward * z + (1 - rightward) * (nz - 1 - z)

    def column(t):
        in_turn = (2 * shorter - t + 2 * nz) // (2 * nz)
        near = (1 - 2 * (t % 2)) * ((t + 1) // 2)
        far = (2 * rightward - 1) * (t - shorter)
        return z + in_turn * near + (1 - in_turn) * far

    def advance(step, carry):
        def part(j, inner):
            yy = other(gray(j))

            @pl.when(z - step >= 0)
            def _():
                arrived(z - step, yy)

                @pl.when(has_right)
                def _():
                    to_right(piece(z - step, yy), z - step, yy).start()

            @pl.when(z + step < nz)
            def _():
                arrived(z + step, yy)

                @pl.when(has_left)
                def _():
                    to_left(piece(z + step, yy), z + step, yy).start()

            @pl.when(jnp.logical_and(step == 1, j > 0))
            def _():
                remote(q_buf.at[yy], q_buf.at[yy], q_recv.at[yy], q_recv.at[yy], device(y, z)).wait_recv()

            attend(yy, column(step - 1))
            return inner

        return lax.fori_loop(0, HEADS, part, carry)

    lax.fori_loop(1, nz, advance, 0)

    def finish(j, carry):
        yq = other(gray(HEADS - 1 - j))
        attend(yq, column(nz - 1))
        out = acc[yq] / jnp.sum(total[yq], axis=-1, keepdims=True)
        out = out.astype(jnp.bfloat16)
        for b in range(2):
            for g in range(GROUP):
                start = (b * GROUP + g) * SPAN
                o_buf[yq, b * SPAN : (b + 1) * SPAN, g * DIM : (g + 1) * DIM] = out[start : start + SPAN]

        @pl.when(j < HEADS - 1)
        def _():
            remote(
                o_buf.at[yq], out_ref.at[:, columns(y)], o_sem.at[yq], o_recv.at[y], device(yq, z)
            ).start()

        return carry

    lax.fori_loop(0, HEADS, finish, 0)
    own_o = pltpu.make_async_copy(o_buf.at[y], out_ref.at[:, columns(y)], own_sem.at[2])
    own_o.start()

    for copy in kv_sends + q_sends:
        copy.wait_send()

    def drain(yy, carry):
        @pl.when(has_right)
        def _():
            def one(zz, inner):
                to_right(piece(zz, yy), zz, yy).wait_send()
                return inner

            lax.fori_loop(0, z + 1, one, 0)

        @pl.when(has_left)
        def _():
            def one(zz, inner):
                to_left(piece(zz, yy), zz, yy).wait_send()
                return inner

            lax.fori_loop(z, nz, one, 0)

        return carry

    lax.fori_loop(0, HEADS, drain, 0)
    for d in (1, 2, 3):
        yy = other(d)
        copy = remote(o_buf.at[yy], out_ref.at[:, columns(yy)], o_sem.at[yy], o_recv.at[yy], device(yy, z))
        copy.wait_send()
        copy.wait_recv()
    own_o.wait()


def per_device(queries, keyvals, span_ids):
    nz = lax.axis_size("ctx") // HEADS
    q = queries[0]
    kv = keyvals[0].reshape(2, SPAN, 2, HEADS, DIM).transpose(3, 2, 0, 1, 4)
    rows = 2 * GROUP * SPAN
    dma = pltpu.SemaphoreType.DMA
    flops = 4 * HEADS * rows * DIM * nz * HEADS * ROWS
    out = pl.pallas_call(
        functools.partial(kernel, nz),
        out_shape=jax.ShapeDtypeStruct(q.shape, jnp.bfloat16),
        in_specs=[
            pl.BlockSpec(memory_space=pltpu.SMEM),
            pl.BlockSpec(memory_space=pl.ANY),
            pl.BlockSpec(memory_space=pl.ANY),
        ],
        out_specs=pl.BlockSpec(memory_space=pl.ANY),
        scratch_shapes=[
            pltpu.VMEM((nz, 2, 2, HEADS, SPAN, DIM), jnp.bfloat16),
            pltpu.VMEM((HEADS, ROWS, GROUP * DIM), jnp.bfloat16),
            pltpu.VMEM((HEADS, ROWS, GROUP * DIM), jnp.bfloat16),
            pltpu.VMEM((nz, 2, SPAN, HEADS * SPAN), jnp.int32),
            pltpu.VMEM((HEADS, rows, DIM), jnp.float32),
            pltpu.VMEM((HEADS, rows, DIM), jnp.float32),
            pltpu.VMEM((HEADS, rows, DIM), jnp.float32),
            dma((nz, HEADS)), dma((nz, HEADS)), dma((nz, HEADS)),
            dma((3,)), dma((3,)), dma((HEADS,)), dma((HEADS,)), dma((HEADS,)), dma((3,)),
        ],
        compiler_params=pltpu.CompilerParams(
            collective_id=0, has_side_effects=True, vmem_limit_bytes=48 * 1024 * 1024
        ),
        cost_estimate=pl.CostEstimate(flops=flops, bytes_accessed=4 * 1024 * 1024, transcendentals=0),
        name="attend",
    )(span_ids, q, kv)
    return out[None]


def solution(mesh):
    in_specs = (P("fsdp", "ctx", None), P("fsdp", "ctx", None, None), P("fsdp", None))
    return jax.shard_map(
        per_device, mesh=mesh, in_specs=in_specs, out_specs=P("fsdp", "ctx", None), check_vma=False
    )
```

```python
import functools
import math

import jax
import jax.numpy as jnp
from jax import lax
from jax.experimental import pallas as pl
from jax.experimental.pallas import tpu as pltpu
from jax.sharding import PartitionSpec as P

HEADS = 4
GROUP = 4
DIM = 128
SPAN = 64
ROWS = 2 * SPAN
NEG = -1e30
MESH = pl.DeviceIdType.MESH
FACTOR = math.log2(math.e) / math.sqrt(DIM)


def gray(j):
    return j + (j // 2) * (5 - 2 * j)


def kernel(
    nz, ids_ref, q_ref, kv_ref, out_ref,
    kv_buf, q_buf, o_buf, gap, acc, total, top,
    recv, right_sem, left_sem, kv_sem, q_sem, q_recv, o_sem, o_recv, own_sem,
):
    me = lax.axis_index("ctx")
    y, z = me // nz, me % nz
    has_left, has_right = z > 0, z < nz - 1
    width = GROUP * DIM
    keys = HEADS * SPAN

    def device(yy, zz):
        return {"ctx": yy * nz + zz}

    def remote(src, dst, send, receive, where):
        return pltpu.make_async_remote_copy(
            src_ref=src, dst_ref=dst, send_sem=send, recv_sem=receive,
            device_id=where, device_id_type=MESH,
        )

    def piece(zz, yy):
        return kv_buf.at[zz, :, :, yy]

    def columns(yy):
        return pl.ds(pl.multiple_of(yy * width, width), width)

    def other(d):
        return (y + d) % HEADS

    barrier = pltpu.get_barrier_semaphore()
    for d in (1, 2, 3):
        pl.semaphore_signal(barrier, inc=1, device_id=device(other(d), z), device_id_type=MESH)

    @pl.when(has_left)
    def _():
        pl.semaphore_signal(barrier, inc=1, device_id=device(y, z - 1), device_id_type=MESH)

    @pl.when(has_right)
    def _():
        pl.semaphore_signal(barrier, inc=1, device_id=device(y, z + 1), device_id_type=MESH)

    pl.semaphore_wait(barrier, 3 + (z + nz - 1) // nz + (2 * nz - 2 - z) // nz)

    def to_right(src, zz, yy):
        return remote(src, piece(zz, yy), right_sem.at[zz, yy], recv.at[zz, yy], device(y, z + 1))

    def to_left(src, zz, yy):
        return remote(src, piece(zz, yy), left_sem.at[zz, yy], recv.at[zz, yy], device(y, z - 1))

    def arrived(zz, yy):
        remote(piece(zz, yy), piece(zz, yy), recv.at[zz, yy], recv.at[zz, yy], device(y, z)).wait_recv()

    @pl.when(has_right)
    def _():
        to_right(kv_ref.at[y], z, y).start()

    @pl.when(has_left)
    def _():
        to_left(kv_ref.at[y], z, y).start()

    kv_sends = [
        remote(kv_ref.at[other(d)], piece(z, y), kv_sem.at[d - 1], recv.at[z, y], device(other(d), z))
        for d in (1, 3, 2)
    ]
    for copy in kv_sends:
        copy.start()
    own_kv = pltpu.make_async_copy(kv_ref.at[y], piece(z, y), own_sem.at[0])
    own_kv.start()
    q_sends = [
        remote(
            q_ref.at[:, columns(other(d))], q_buf.at[y], q_sem.at[d - 1], q_recv.at[y], device(other(d), z)
        )
        for d in (1, 3, 2)
    ]
    for copy in q_sends:
        copy.start()
    own_q = pltpu.make_async_copy(q_ref.at[:, columns(y)], q_buf.at[y], own_sem.at[1])
    own_q.start()

    for d in (1, 3, 2):
        arrived(z, other(d))

        @pl.when(has_right)
        def _():
            to_right(piece(z, other(d)), z, other(d)).start()

        @pl.when(has_left)
        def _():
            to_left(piece(z, other(d)), z, other(d)).start()

    lane = lax.broadcasted_iota(jnp.int32, (SPAN, keys), 1)
    row = lax.broadcasted_iota(jnp.int32, (SPAN, keys), 0)
    base = lane % SPAN - row

    def fill(zz, carry):
        for half in range(2):
            span = jnp.zeros((SPAN, keys), jnp.int32)
            for yy in range(HEADS):
                span = jnp.where(lane // SPAN == yy, ids_ref[0, 2 * (yy * nz + zz) + half], span)
            gap[zz, half] = span * SPAN + base
        return carry

    lax.fori_loop(0, nz, fill, 0)
    top[...] = jnp.full(top.shape, NEG, jnp.float32)
    total[...] = jnp.zeros(total.shape, jnp.float32)
    acc[...] = jnp.zeros(acc.shape, jnp.float32)
    own_kv.wait()
    own_q.wait()

    def product(a, b):
        return lax.dot_general(a, b, (((1,), (1,)), ((), ())), preferred_element_type=jnp.float32)

    def soften(yq, rows, scores):
        best = scores[0]
        for s in scores[1:]:
            best = jnp.maximum(best, s)
        old = top[yq, rows]
        new = jnp.maximum(old, jnp.max(best, axis=-1, keepdims=True))
        shrink = jnp.exp2((old - new) * FACTOR)
        wide = jnp.concatenate([new] * (keys // DIM), axis=-1)
        summed = total[yq, rows] * shrink
        weights = []
        for s in scores:
            p = jnp.exp2((s - wide) * FACTOR)
            for k in range(keys // DIM):
                summed = summed + p[:, k * DIM : (k + 1) * DIM]
            weights.append(p.astype(jnp.bfloat16))
        total[yq, rows] = summed
        top[yq, rows] = new
        return weights, shrink

    def attend(yqs, zz):
        low_k, high_k, low_v, high_v = (
            kv_buf[zz, a, b].reshape(keys, DIM) for a in range(2) for b in range(2)
        )
        lows, highs = (
            [
                q_buf[yq, b * SPAN : (b + 1) * SPAN, g * DIM : (g + 1) * DIM]
                for yq in yqs
                for g in range(GROUP)
            ]
            for b in range(2)
        )
        half = GROUP * SPAN
        rows = len(yqs) * half
        by_low = product(jnp.concatenate(lows + highs, axis=0), low_k)
        by_high = product(jnp.concatenate(highs, axis=0), high_k)

        def masked(s, yq, b):
            distance = jnp.concatenate([gap[zz, b]] * GROUP, axis=0)
            return jnp.where(distance <= ids_ref[0, 2 * (yq * nz + z) + b] * SPAN, s, NEG)

        p_low, p_high_low, p_high, shrinks = [], [], [], []
        for n, yq in enumerate(yqs):
            part = slice(n * half, (n + 1) * half)
            (p,), shrink_low = soften(yq, pl.ds(0, half), [masked(by_low[part], yq, 0)])
            scores = [by_low[rows + n * half : rows + (n + 1) * half], masked(by_high[part], yq, 1)]
            (p1, p2), shrink_high = soften(yq, pl.ds(half, half), scores)
            p_low.append(p)
            p_high_low.append(p1)
            p_high.append(p2)
            shrinks.append((shrink_low, shrink_high))
        from_low = jnp.dot(jnp.concatenate(p_low + p_high_low, axis=0), low_v, preferred_element_type=jnp.float32)
        from_high = jnp.dot(jnp.concatenate(p_high, axis=0), high_v, preferred_element_type=jnp.float32)
        for n, yq in enumerate(yqs):
            part = slice(n * half, (n + 1) * half)
            acc[yq, pl.ds(0, half)] = acc[yq, pl.ds(0, half)] * shrinks[n][0] + from_low[part]
            acc[yq, pl.ds(half, half)] = (
                acc[yq, pl.ds(half, half)] * shrinks[n][1]
                + from_low[rows + n * half : rows + (n + 1) * half]
                + from_high[part]
            )

    rightward = (3 * nz - 2 - 2 * z) // (2 * nz)
    shorter = rightward * z + (1 - rightward) * (nz - 1 - z)

    def column(t):
        in_turn = (2 * shorter - t + 2 * nz) // (2 * nz)
        near = (1 - 2 * (t % 2)) * ((t + 1) // 2)
        far = (2 * rightward - 1) * (t - shorter)
        return z + in_turn * near + (1 - in_turn) * far

    def advance(step, carry):
        def part(j, inner):
            yy = other(gray(j))

            @pl.when(z - step >= 0)
            def _():
                arrived(z - step, yy)

                @pl.when(has_right)
                def _():
                    to_right(piece(z - step, yy), z - step, yy).start()

            @pl.when(z + step < nz)
            def _():
                arrived(z + step, yy)

                @pl.when(has_left)
                def _():
                    to_left(piece(z + step, yy), z + step, yy).start()

            @pl.when(jnp.logical_and(step == 1, j > 0))
            def _():
                remote(q_buf.at[yy], q_buf.at[yy], q_recv.at[yy], q_recv.at[yy], device(y, z)).wait_recv()

            @pl.when(j % 2 == 1)
            def _():
                attend([other(gray(j - 1)), yy], column(step - 1))

            return inner

        return lax.fori_loop(0, HEADS, part, carry)

    lax.fori_loop(1, nz, advance, 0)

    def finish(j, carry):
        yq = other(gray(HEADS - 1 - j))

        @pl.when(j % 2 == 0)
        def _():
            attend([yq, other(gray(HEADS - 2 - j))], column(nz - 1))

        out = acc[yq] / jnp.sum(total[yq], axis=-1, keepdims=True)
        out = out.astype(jnp.bfloat16)
        for b in range(2):
            for g in range(GROUP):
                start = (b * GROUP + g) * SPAN
                o_buf[yq, b * SPAN : (b + 1) * SPAN, g * DIM : (g + 1) * DIM] = out[start : start + SPAN]

        @pl.when(j < HEADS - 1)
        def _():
            remote(
                o_buf.at[yq], out_ref.at[:, columns(y)], o_sem.at[yq], o_recv.at[y], device(yq, z)
            ).start()

        return carry

    lax.fori_loop(0, HEADS, finish, 0)
    own_o = pltpu.make_async_copy(o_buf.at[y], out_ref.at[:, columns(y)], own_sem.at[2])
    own_o.start()

    for copy in kv_sends + q_sends:
        copy.wait_send()

    def drain(yy, carry):
        @pl.when(has_right)
        def _():
            def one(zz, inner):
                to_right(piece(zz, yy), zz, yy).wait_send()
                return inner

            lax.fori_loop(0, z + 1, one, 0)

        @pl.when(has_left)
        def _():
            def one(zz, inner):
                to_left(piece(zz, yy), zz, yy).wait_send()
                return inner

            lax.fori_loop(z, nz, one, 0)

        return carry

    lax.fori_loop(0, HEADS, drain, 0)
    for d in (1, 2, 3):
        yy = other(d)
        copy = remote(o_buf.at[yy], out_ref.at[:, columns(yy)], o_sem.at[yy], o_recv.at[yy], device(yy, z))
        copy.wait_send()
        copy.wait_recv()
    own_o.wait()


def per_device(queries, keyvals, span_ids):
    nz = lax.axis_size("ctx") // HEADS
    q = queries[0]
    kv = keyvals[0].reshape(2, SPAN, 2, HEADS, DIM).transpose(3, 2, 0, 1, 4)
    rows = 2 * GROUP * SPAN
    dma = pltpu.SemaphoreType.DMA
    flops = 4 * HEADS * rows * DIM * nz * HEADS * ROWS
    out = pl.pallas_call(
        functools.partial(kernel, nz),
        out_shape=jax.ShapeDtypeStruct(q.shape, jnp.bfloat16),
        in_specs=[
            pl.BlockSpec(memory_space=pltpu.SMEM),
            pl.BlockSpec(memory_space=pl.ANY),
            pl.BlockSpec(memory_space=pl.ANY),
        ],
        out_specs=pl.BlockSpec(memory_space=pl.ANY),
        scratch_shapes=[
            pltpu.VMEM((nz, 2, 2, HEADS, SPAN, DIM), jnp.bfloat16),
            pltpu.VMEM((HEADS, ROWS, GROUP * DIM), jnp.bfloat16),
            pltpu.VMEM((HEADS, ROWS, GROUP * DIM), jnp.bfloat16),
            pltpu.VMEM((nz, 2, SPAN, HEADS * SPAN), jnp.int32),
            pltpu.VMEM((HEADS, rows, DIM), jnp.float32),
            pltpu.VMEM((HEADS, rows, DIM), jnp.float32),
            pltpu.VMEM((HEADS, rows, DIM), jnp.float32),
            dma((nz, HEADS)), dma((nz, HEADS)), dma((nz, HEADS)),
            dma((3,)), dma((3,)), dma((HEADS,)), dma((HEADS,)), dma((HEADS,)), dma((3,)),
        ],
        compiler_params=pltpu.CompilerParams(
            collective_id=0, has_side_effects=True, vmem_limit_bytes=48 * 1024 * 1024
        ),
        cost_estimate=pl.CostEstimate(flops=flops, bytes_accessed=4 * 1024 * 1024, transcendentals=0),
        name="attend",
    )(span_ids, q, kv)
    return out[None]


def solution(mesh):
    in_specs = (P("fsdp", "ctx", None), P("fsdp", "ctx", None, None), P("fsdp", None))
    return jax.shard_map(
        per_device, mesh=mesh, in_specs=in_specs, out_specs=P("fsdp", "ctx", None), check_vma=False
    )
```

```python
import functools
import math

import jax
import jax.numpy as jnp
from jax import lax
from jax.experimental import pallas as pl
from jax.experimental.pallas import tpu as pltpu
from jax.sharding import PartitionSpec as P

HEADS = 4
GROUP = 4
DIM = 128
SPAN = 64
ROWS = 2 * SPAN
NEG = -1e30
MESH = pl.DeviceIdType.MESH
FACTOR = math.log2(math.e) / math.sqrt(DIM)


def gray(j):
    return j + (j // 2) * (5 - 2 * j)


def kernel(
    nz, ids_in, q_ref, kv_ref, out_ref,
    ids_ref, kv_buf, q_buf, o_buf, gap, acc, total, top,
    recv, right_sem, left_sem, kv_sem, q_sem, q_recv, o_sem, o_recv, own_sem,
):
    me = lax.axis_index("ctx")
    y, z = me // nz, me % nz
    has_left, has_right = z > 0, z < nz - 1
    width = GROUP * DIM
    keys = HEADS * SPAN

    def device(yy, zz):
        return {"ctx": yy * nz + zz}

    def remote(src, dst, send, receive, where):
        return pltpu.make_async_remote_copy(
            src_ref=src, dst_ref=dst, send_sem=send, recv_sem=receive,
            device_id=where, device_id_type=MESH,
        )

    def piece(zz, yy):
        return kv_buf.at[zz, :, :, yy]

    def columns(yy):
        return pl.ds(pl.multiple_of(yy * width, width), width)

    def other(d):
        return (y + d) % HEADS

    barrier = pltpu.get_barrier_semaphore()
    for d in (1, 2, 3):
        pl.semaphore_signal(barrier, inc=1, device_id=device(other(d), z), device_id_type=MESH)

    @pl.when(has_left)
    def _():
        pl.semaphore_signal(barrier, inc=1, device_id=device(y, z - 1), device_id_type=MESH)

    @pl.when(has_right)
    def _():
        pl.semaphore_signal(barrier, inc=1, device_id=device(y, z + 1), device_id_type=MESH)

    pl.semaphore_wait(barrier, 3 + (z + nz - 1) // nz + (2 * nz - 2 - z) // nz)

    def to_right(src, zz, yy):
        return remote(src, piece(zz, yy), right_sem.at[zz, yy], recv.at[zz, yy], device(y, z + 1))

    def to_left(src, zz, yy):
        return remote(src, piece(zz, yy), left_sem.at[zz, yy], recv.at[zz, yy], device(y, z - 1))

    def arrived(zz, yy):
        remote(piece(zz, yy), piece(zz, yy), recv.at[zz, yy], recv.at[zz, yy], device(y, z)).wait_recv()

    @pl.when(has_right)
    def _():
        to_right(kv_ref.at[y], z, y).start()

    @pl.when(has_left)
    def _():
        to_left(kv_ref.at[y], z, y).start()

    kv_sends = [
        remote(kv_ref.at[other(d)], piece(z, y), kv_sem.at[d - 1], recv.at[z, y], device(other(d), z))
        for d in (2, 1, 3)
    ]
    for copy in kv_sends:
        copy.start()
    ids_copy = pltpu.make_async_copy(ids_in, ids_ref, own_sem.at[3])
    ids_copy.start()
    own_kv = pltpu.make_async_copy(kv_ref.at[y], piece(z, y), own_sem.at[0])
    own_kv.start()
    q_sends = [
        remote(
            q_ref.at[:, columns(other(d))], q_buf.at[y], q_sem.at[d - 1], q_recv.at[y], device(other(d), z)
        )
        for d in (1, 3, 2)
    ]
    for copy in q_sends:
        copy.start()
    own_q = pltpu.make_async_copy(q_ref.at[:, columns(y)], q_buf.at[y], own_sem.at[1])
    own_q.start()

    for d in (1, 3, 2):
        arrived(z, other(d))

        @pl.when(has_right)
        def _():
            to_right(piece(z, other(d)), z, other(d)).start()

        @pl.when(has_left)
        def _():
            to_left(piece(z, other(d)), z, other(d)).start()

    ids_copy.wait()

    lane = lax.broadcasted_iota(jnp.int32, (SPAN, keys), 1)
    row = lax.broadcasted_iota(jnp.int32, (SPAN, keys), 0)
    base = lane % SPAN - row

    def fill(zz, carry):
        for half in range(2):
            span = jnp.zeros((SPAN, keys), jnp.int32)
            for yy in range(HEADS):
                span = jnp.where(lane // SPAN == yy, ids_ref[0, 2 * (yy * nz + zz) + half], span)
            gap[zz, half] = span * SPAN + base
        return carry

    lax.fori_loop(0, nz, fill, 0)
    top[...] = jnp.full(top.shape, NEG, jnp.float32)
    total[...] = jnp.zeros(total.shape, jnp.float32)
    acc[...] = jnp.zeros(acc.shape, jnp.float32)
    own_kv.wait()
    own_q.wait()

    def product(a, b):
        return lax.dot_general(a, b, (((1,), (1,)), ((), ())), preferred_element_type=jnp.float32)

    def soften(yq, rows, scores):
        best = scores[0]
        for s in scores[1:]:
            best = jnp.maximum(best, s)
        old = top[yq, rows]
        new = jnp.maximum(old, jnp.max(best, axis=-1, keepdims=True))
        shrink = jnp.exp2((old - new) * FACTOR)
        wide = jnp.concatenate([new] * (keys // DIM), axis=-1)
        summed = total[yq, rows] * shrink
        weights = []
        for s in scores:
            p = jnp.exp2((s - wide) * FACTOR)
            for k in range(keys // DIM):
                summed = summed + p[:, k * DIM : (k + 1) * DIM]
            weights.append(p.astype(jnp.bfloat16))
        total[yq, rows] = summed
        top[yq, rows] = new
        return weights, shrink

    def attend(yqs, zz):
        low_k, high_k, low_v, high_v = (
            kv_buf[zz, a, b].reshape(keys, DIM) for a in range(2) for b in range(2)
        )
        lows, highs = (
            [
                q_buf[yq, b * SPAN : (b + 1) * SPAN, g * DIM : (g + 1) * DIM]
                for yq in yqs
                for g in range(GROUP)
            ]
            for b in range(2)
        )
        half = GROUP * SPAN
        rows = len(yqs) * half
        by_low = product(jnp.concatenate(lows + highs, axis=0), low_k)
        by_high = product(jnp.concatenate(highs, axis=0), high_k)

        def masked(s, yq, b):
            distance = jnp.concatenate([gap[zz, b]] * GROUP, axis=0)
            return jnp.where(distance <= ids_ref[0, 2 * (yq * nz + z) + b] * SPAN, s, NEG)

        p_low, p_high_low, p_high, shrinks = [], [], [], []
        for n, yq in enumerate(yqs):
            part = slice(n * half, (n + 1) * half)
            (p,), shrink_low = soften(yq, pl.ds(0, half), [masked(by_low[part], yq, 0)])
            scores = [by_low[rows + n * half : rows + (n + 1) * half], masked(by_high[part], yq, 1)]
            (p1, p2), shrink_high = soften(yq, pl.ds(half, half), scores)
            p_low.append(p)
            p_high_low.append(p1)
            p_high.append(p2)
            shrinks.append((shrink_low, shrink_high))
        from_low = jnp.dot(jnp.concatenate(p_low + p_high_low, axis=0), low_v, preferred_element_type=jnp.float32)
        from_high = jnp.dot(jnp.concatenate(p_high, axis=0), high_v, preferred_element_type=jnp.float32)
        for n, yq in enumerate(yqs):
            part = slice(n * half, (n + 1) * half)
            acc[yq, pl.ds(0, half)] = acc[yq, pl.ds(0, half)] * shrinks[n][0] + from_low[part]
            acc[yq, pl.ds(half, half)] = (
                acc[yq, pl.ds(half, half)] * shrinks[n][1]
                + from_low[rows + n * half : rows + (n + 1) * half]
                + from_high[part]
            )

    rightward = (3 * nz - 2 - 2 * z) // (2 * nz)
    shorter = rightward * z + (1 - rightward) * (nz - 1 - z)

    def column(t):
        in_turn = (2 * shorter - t + 2 * nz) // (2 * nz)
        near = (1 - 2 * (t % 2)) * ((t + 1) // 2)
        far = (2 * rightward - 1) * (t - shorter)
        return z + in_turn * near + (1 - in_turn) * far

    def advance(step, carry):
        def part(j, inner):
            yy = other(gray(j))

            @pl.when(z - step >= 0)
            def _():
                arrived(z - step, yy)

                @pl.when(has_right)
                def _():
                    to_right(piece(z - step, yy), z - step, yy).start()

            @pl.when(z + step < nz)
            def _():
                arrived(z + step, yy)

                @pl.when(has_left)
                def _():
                    to_left(piece(z + step, yy), z + step, yy).start()

            @pl.when(jnp.logical_and(step == 1, j > 0))
            def _():
                remote(q_buf.at[yy], q_buf.at[yy], q_recv.at[yy], q_recv.at[yy], device(y, z)).wait_recv()

            @pl.when(j % 2 == 1)
            def _():
                attend([other(gray(j - 1)), yy], column(step - 1))

            return inner

        return lax.fori_loop(0, HEADS, part, carry)

    lax.fori_loop(1, nz, advance, 0)

    def finish(j, carry):
        yq = other(gray(HEADS - 1 - j))

        @pl.when(j % 2 == 0)
        def _():
            attend([yq, other(gray(HEADS - 2 - j))], column(nz - 1))

        out = acc[yq] / jnp.sum(total[yq], axis=-1, keepdims=True)
        out = out.astype(jnp.bfloat16)
        for b in range(2):
            for g in range(GROUP):
                start = (b * GROUP + g) * SPAN
                o_buf[yq, b * SPAN : (b + 1) * SPAN, g * DIM : (g + 1) * DIM] = out[start : start + SPAN]

        @pl.when(j < HEADS - 1)
        def _():
            remote(
                o_buf.at[yq], out_ref.at[:, columns(y)], o_sem.at[yq], o_recv.at[y], device(yq, z)
            ).start()

        return carry

    lax.fori_loop(0, HEADS, finish, 0)
    own_o = pltpu.make_async_copy(o_buf.at[y], out_ref.at[:, columns(y)], own_sem.at[2])
    own_o.start()

    for copy in kv_sends + q_sends:
        copy.wait_send()

    def drain(yy, carry):
        @pl.when(has_right)
        def _():
            def one(zz, inner):
                to_right(piece(zz, yy), zz, yy).wait_send()
                return inner

            lax.fori_loop(0, z + 1, one, 0)

        @pl.when(has_left)
        def _():
            def one(zz, inner):
                to_left(piece(zz, yy), zz, yy).wait_send()
                return inner

            lax.fori_loop(z, nz, one, 0)

        return carry

    lax.fori_loop(0, HEADS, drain, 0)
    for d in (1, 2, 3):
        yy = other(d)
        copy = remote(o_buf.at[yy], out_ref.at[:, columns(yy)], o_sem.at[yy], o_recv.at[yy], device(yy, z))
        copy.wait_send()
        copy.wait_recv()
    own_o.wait()


def per_device(queries, keyvals, span_ids):
    nz = lax.axis_size("ctx") // HEADS
    q = queries[0]
    kv = keyvals[0].reshape(2, SPAN, 2, HEADS, DIM).transpose(3, 2, 0, 1, 4)
    rows = 2 * GROUP * SPAN
    dma = pltpu.SemaphoreType.DMA
    flops = 4 * HEADS * rows * DIM * nz * HEADS * ROWS
    out = pl.pallas_call(
        functools.partial(kernel, nz),
        out_shape=jax.ShapeDtypeStruct(q.shape, jnp.bfloat16),
        in_specs=[
            pl.BlockSpec(memory_space=pltpu.HBM),
            pl.BlockSpec(memory_space=pl.ANY),
            pl.BlockSpec(memory_space=pl.ANY),
        ],
        out_specs=pl.BlockSpec(memory_space=pl.ANY),
        scratch_shapes=[
            pltpu.SMEM(span_ids.shape, jnp.int32),
            pltpu.VMEM((nz, 2, 2, HEADS, SPAN, DIM), jnp.bfloat16),
            pltpu.VMEM((HEADS, ROWS, GROUP * DIM), jnp.bfloat16),
            pltpu.VMEM((HEADS, ROWS, GROUP * DIM), jnp.bfloat16),
            pltpu.VMEM((nz, 2, SPAN, HEADS * SPAN), jnp.int32),
            pltpu.VMEM((HEADS, rows, DIM), jnp.float32),
            pltpu.VMEM((HEADS, rows, DIM), jnp.float32),
            pltpu.VMEM((HEADS, rows, DIM), jnp.float32),
            dma((nz, HEADS)), dma((nz, HEADS)), dma((nz, HEADS)),
            dma((3,)), dma((3,)), dma((HEADS,)), dma((HEADS,)), dma((HEADS,)), dma((4,)),
        ],
        compiler_params=pltpu.CompilerParams(
            collective_id=0, has_side_effects=True, vmem_limit_bytes=60 * 1024 * 1024
        ),
        cost_estimate=pl.CostEstimate(flops=flops, bytes_accessed=4 * 1024 * 1024, transcendentals=0),
        name="attend",
    )(span_ids, q, kv)
    return out[None]


def solution(mesh):
    in_specs = (P("fsdp", "ctx", None), P("fsdp", "ctx", None, None), P("fsdp", None))
    return jax.shard_map(
        per_device, mesh=mesh, in_specs=in_specs, out_specs=P("fsdp", "ctx", None), check_vma=False
    )
```
